256 devices in a mesh: ctx: 32 (over z, x), ch: 8 (over y, core).
Axes of the slice: x: 4, y: 4, z: 8, core: 2. Of those that a mesh axis runs over, the one named last changes fastest.
Arguments:
- query_input: bfloat16 [4096, 4096], P('ctx', 'ch'), may hold values from -6 to 6
- key_input: bfloat16 [4096, 4096], P('ctx', 'ch'), may hold values from -6 to 6
- value_input: bfloat16 [4096, 4096], P('ctx', 'ch'), may hold values from -6 to 6
- short_weight: float32 [3, 3, 4096], P(None, None, 'ch'), may hold values from -3.5 to 3.5
- residue: float32 [16, 4096], P(None, 'ch'), may hold values from -1.5 to 1.5
- decay_rate: float32 [16, 4096], P(None, 'ch'), may hold values from 0.00012207031 to 0.05
- skip_gain: float32 [4096], P('ch'), may hold values from -1 to 1
- out_weight: bfloat16 [4096, 8192], P('ch'), may hold values from -0.125 to 0.125
Outputs:
- layer_output: bfloat16 [4096, 8192], P('ctx', 'ch')
The draws below stay inside these ranges and needn't reach their ends.
All inputs are finite; a program needn't handle non-finite values.
Results may differ from the reference program's by a relative error of at most 0.015.
Values may be sent and summed in bfloat16 or wider, within the bound.
No kernel may reach another device: no remote copies, remote signals or barrier semaphores. Data moves between devices by JAX's collectives and lax.ppermute only.
A program may use at most 64 MiB of HBM per device.

```python
import math
import jax
import jax.numpy as jnp

D = 8192
DH = 4096
ORDER = 16
TAPS = 3
TOKENS = 4096


def spiked(entries, key, source, target, parts, factor):
    owner, partner = [(jnp.arange(entries.shape[position]) // (entries.shape[position] // parts)).reshape([-1 if axis == position else 1 for axis in range(entries.ndim)]) for position in (source, target)]
    chosen = jax.random.permutation(key, parts)[partner]
    strong = (owner == chosen) | (owner == (partner + parts // 2) % parts)
    return jnp.where(strong, factor * entries, entries)


def block_scale(key, shape, pieces, smallest, largest):
    loudness = 1.0
    for axis_at, shards_of in pieces:
        heights = jax.random.uniform(jax.random.fold_in(jax.random.fold_in(key, 6), axis_at), (shards_of,), jnp.float32, smallest / len(pieces), largest / len(pieces))
        loudness = loudness * jnp.repeat(jnp.exp(heights), shape[axis_at] // shards_of).reshape((-1,) + (1,) * (len(shape) - 1 - axis_at))
    return loudness


def normal_values(stream_key, extent, spread, reach, pieces=(), held_as=jnp.bfloat16):
    gain = block_scale(stream_key, extent, pieces, -0.22, 0.18) if pieces else 1.0
    array = jax.random.normal(stream_key, extent, jnp.float32) * spread * gain
    return jnp.minimum(jnp.maximum(array, -reach), reach).astype(held_as)


def gaussian_with(stream_key, extent, scale, most, split, heavy, kind=jnp.bfloat16):
    drawn = scale * jax.random.normal(stream_key, extent, jnp.float32)
    if split:
        drawn = drawn * block_scale(stream_key, extent, split, -0.22, 0.18)
    return jnp.clip(spiked(drawn, jax.random.fold_in(stream_key, 3), *heavy), -most, most).astype(kind)


def setup_inputs(seed: int = 0) -> dict:
    arg_keys = jax.random.split(jax.random.key(seed), 9)
    return {
        "query_input": normal_values(arg_keys[0], (TOKENS, DH), 1.0, 6.0, ((0, 32), (1, 8))),
        "key_input": normal_values(arg_keys[1], (TOKENS, DH), 1.0, 6.0, ((0, 32), (1, 8))),
        "value_input": normal_values(arg_keys[2], (TOKENS, DH), 1.0, 6.0, ((0, 32), (1, 8))),
        "short_weight": normal_values(arg_keys[3], (3, TAPS, DH), TAPS ** -0.5, 3.5, ((2, 8),), jnp.float32),
        "residue": normal_values(arg_keys[4], (ORDER, DH), 0.25, 1.5, ((1, 8),), jnp.float32),
        "decay_rate": jnp.clip(jnp.exp(math.log(0.05) - 6.015181 * jax.random.uniform(arg_keys[5], (ORDER, DH), jnp.float32) ** block_scale(arg_keys[5], (ORDER, DH), ((1, 8),), -0.2, 0.2)), 0.00012207031, 0.05),
        "skip_gain": jnp.clip(jax.random.uniform(arg_keys[6], (DH,), jnp.float32, -1.0, 1.0) * block_scale(arg_keys[6], (DH,), ((0, 8),), -0.4, 0.0), -1.0, 1.0),
        "out_weight": gaussian_with(arg_keys[7], (DH, D), DH ** -0.5, 0.125, ((0, 8),), (0, 1, 8, 2.0)),
    }


def filter_block(residue, decay_rate, first_row, row_count):
    moments = (first_row + jnp.arange(row_count, dtype=jnp.int32)).astype(jnp.float32)[:, None]
    running = jnp.zeros((row_count, residue.shape[1]), jnp.float32)
    for order_mode in range(residue.shape[0]):
        running = running + residue[order_mode] * jnp.sqrt(2.0 * decay_rate[order_mode]) * jnp.exp(-decay_rate[order_mode] * moments)
    return running

def short_filter(raw_rows, prior_rows, taps):
    extended = jnp.concatenate([prior_rows, raw_rows], axis=0).astype(jnp.float32)
    length_rows = raw_rows.shape[0]
    tap_count = taps.shape[0]
    running = jnp.zeros(raw_rows.shape, jnp.float32)
    for offset in range(tap_count):
        running = running + taps[offset] * extended[tap_count - 1 - offset:tap_count - 1 - offset + length_rows]
    return running

def reference(query_input, key_input, value_input, short_weight, residue, decay_rate, skip_gain, out_weight):
    prior_zero = jnp.zeros((TAPS - 1, DH), jnp.bfloat16)
    query_conv = short_filter(query_input, prior_zero, short_weight[0])
    key_conv = short_filter(key_input, prior_zero, short_weight[1])
    value_conv = short_filter(value_input, prior_zero, short_weight[2])
    mixed_input = key_conv * value_conv
    impulse = filter_block(residue, decay_rate, 0, TOKENS)
    spectrum = jnp.fft.rfft(mixed_input, n=2 * TOKENS, axis=0) * jnp.fft.rfft(impulse, n=2 * TOKENS, axis=0)
    convolved = jnp.fft.irfft(spectrum, n=2 * TOKENS, axis=0)[:TOKENS].astype(jnp.float32)
    gated = (query_conv * (convolved + skip_gain * mixed_input)).astype(jnp.bfloat16)
    return jnp.dot(gated, out_weight, preferred_element_type=jnp.float32).astype(jnp.bfloat16)
```

```python
import functools

import jax
import jax.numpy as jnp
from jax import lax
from jax.experimental import pallas as pl
from jax.experimental.pallas import tpu as pltpu
from jax.sharding import PartitionSpec as P

F32 = jnp.float32
BF16 = jnp.bfloat16
SUBLANES = 8
LANES = 128


def rows_of(shape):
    return lax.broadcasted_iota(jnp.int32, shape, 0)


def short_conv(raw, prior, taps):
    x = raw.astype(F32)
    row = rows_of(x.shape)
    older = prior[0:1].astype(F32)
    newer = prior[1:2].astype(F32)
    back1 = jnp.where(row == 0, newer, pltpu.roll(x, 1, axis=0))
    back2 = jnp.where(
        row == 0, older, jnp.where(row == 1, newer, pltpu.roll(x, 2, axis=0))
    )
    return taps[0:1] * x + taps[1:2] * back1 + taps[2:3] * back2


def spread(row):
    return jnp.broadcast_to(row, (SUBLANES, row.shape[-1]))


def state_kernel(k_ref, v_ref, halo_ref, taps_ref, rate_ref, state_ref, ends_ref, mixed):
    modes, width = rate_ref.shape
    steps = k_ref.shape[0] // SUBLANES
    product = short_conv(k_ref[...], halo_ref[0:2], taps_ref[1]) * short_conv(
        v_ref[...], halo_ref[2:4], taps_ref[2]
    )
    for at in range(0, width, LANES):
        mixed[at // LANES] = product[:, at : at + LANES]
    left = (SUBLANES - 1 - rows_of((SUBLANES, LANES))).astype(F32) * float(steps)
    for at in range(0, width, LANES):
        cols = pl.ds(at, LANES)
        rate = rate_ref[:, cols]
        decay = jnp.exp(-rate)
        keep = [spread(decay[r : r + 1]) for r in range(modes)]
        held = [mixed[at // LANES, pl.ds(0, SUBLANES, steps), :]] * modes
        for a in range(1, steps):
            fresh = mixed[at // LANES, pl.ds(a, SUBLANES, steps), :]
            held = [keep[r] * held[r] + fresh for r in range(modes)]
        totals = []
        for r in range(modes):
            ends_ref[r, :, cols] = held[r]
            weight = jnp.exp(-spread(rate[r : r + 1]) * left)
            totals.append(jnp.sum(weight * held[r], axis=0, keepdims=True))
        state_ref[:, cols] = jnp.concatenate(totals, axis=0).astype(state_ref.dtype)


def gate_kernel(
    ctx_ref, q_ref, k_ref, v_ref, halo_ref, taps_ref, residue_ref, rate_ref, skip_ref,
    states_ref, ends_ref, gated_ref, mixed, carry, convolved,
):
    modes, width = rate_ref.shape
    rows = k_ref.shape[0]
    steps = rows // SUBLANES
    product = short_conv(k_ref[...], halo_ref[0:2], taps_ref[1]) * short_conv(
        v_ref[...], halo_ref[2:4], taps_ref[2]
    )
    for at in range(0, width, LANES):
        mixed[at // LANES] = product[:, at : at + LANES]
    across = jnp.exp(-rate_ref[...] * float(rows))

    def add_block(j, total):
        return across * total + states_ref[j].astype(F32)

    carry[...] = lax.fori_loop(0, ctx_ref[0], add_block, jnp.zeros((modes, width), F32))
    seg = rows_of((SUBLANES, LANES))
    for at in range(0, width, LANES):
        cols = pl.ds(at, LANES)
        rate = rate_ref[:, cols]
        decay = jnp.exp(-rate)
        skip1 = jnp.exp(-rate * float(steps))
        skip2 = skip1 * skip1
        skip4 = skip2 * skip2
        gain = residue_ref[:, cols] * jnp.sqrt(2.0 * rate)
        begin = carry[:, cols]
        held = []
        for r in range(modes):
            one = slice(r, r + 1)
            h = jnp.where(seg == 0, spread(begin[one]), pltpu.roll(ends_ref[r, :, cols], 1, axis=0))
            for apart, factor in ((1, skip1), (2, skip2), (4, skip4)):
                h = h + jnp.where(seg >= apart, spread(factor[one]), 0.0) * pltpu.roll(h, apart, axis=0)
            held.append(h)
        keep = [spread(decay[r : r + 1]) for r in range(modes)]
        gains = [spread(gain[r : r + 1]) for r in range(modes)]
        for a in range(steps):
            picked = pl.ds(a, SUBLANES, steps)
            fresh = mixed[at // LANES, picked, :]
            held = [keep[r] * held[r] + fresh for r in range(modes)]
            terms = [gains[r] * held[r] for r in range(modes)]
            while len(terms) > 1:
                terms = [x + y for x, y in zip(terms[::2], terms[1::2])]
            convolved[at // LANES, picked, :] = terms[0]
    query = short_conv(q_ref[...], halo_ref[4:6], taps_ref[0])
    for at in range(0, width, LANES):
        cols = pl.ds(at, LANES)
        long = convolved[at // LANES] + skip_ref[:, cols] * mixed[at // LANES]
        gated_ref[:, cols] = (query[:, at : at + LANES] * long).astype(gated_ref.dtype)


def project_kernel(order_ref, gated_ref, weight_ref, out_ref):
    out_ref[...] = jnp.dot(gated_ref[...], weight_ref[...], preferred_element_type=F32).astype(
        out_ref.dtype
    )


def project_add_kernel(order_ref, gated_ref, weight_ref, other_ref, out_ref):
    out_ref[...] = (
        jnp.dot(gated_ref[...], weight_ref[...], preferred_element_type=F32)
        + other_ref[...].astype(F32)
    ).astype(out_ref.dtype)


def project(order, gated, weight, width, other=None, dtype=BF16):
    rows, depth = gated.shape
    count = order.shape[0]
    specs = [
        pl.BlockSpec((rows, depth), lambda i, o: (0, 0)),
        pl.BlockSpec((depth, width), lambda i, o: (0, o[i])),
    ]
    operands = [order, gated, weight]
    if other is not None:
        specs.append(pl.BlockSpec((rows, width), lambda i, o: (i, 0)))
        operands.append(other)
    return pl.pallas_call(
        project_kernel if other is None else project_add_kernel,
        out_shape=jax.ShapeDtypeStruct((count * rows, width), dtype),
        grid_spec=pltpu.PrefetchScalarGridSpec(
            num_scalar_prefetch=1,
            grid=(count,),
            in_specs=specs,
            out_specs=pl.BlockSpec((rows, width), lambda i, o: (i, 0)),
        ),
        cost_estimate=pl.CostEstimate(
            flops=2 * rows * depth * width * count,
            bytes_accessed=2 * count * width * (depth + rows),
            transcendentals=0,
        ),
    )(*operands)


def body(
    query_input, key_input, value_input, short_weight, residue, decay_rate, skip_gain, out_weight
):
    ctx = lax.axis_index("ctx")
    blocks = lax.axis_size("ctx")
    ch = lax.axis_index("ch")
    parts = lax.axis_size("ch")
    chips = parts // 2
    rows, width = query_input.shape
    modes = residue.shape[0]
    last = rows - (short_weight.shape[1] - 1)
    edge = jnp.concatenate(
        [key_input[last:], value_input[last:], query_input[last:], query_input[last:]], axis=0
    )
    halo = lax.ppermute(edge, "ctx", [(i, i + 1) for i in range(blocks - 1)])

    whole = pl.BlockSpec(memory_space=pltpu.VMEM)
    state, ends = pl.pallas_call(
        state_kernel,
        out_shape=(
            jax.ShapeDtypeStruct((modes, width), BF16),
            jax.ShapeDtypeStruct((modes, SUBLANES, width), F32),
        ),
        in_specs=[whole] * 5,
        out_specs=(whole, whole),
        scratch_shapes=[pltpu.VMEM((width // LANES, rows, LANES), F32)],
    )(key_input, value_input, halo, short_weight, decay_rate)

    states = lax.all_to_all(
        jnp.broadcast_to(state[None], (blocks, modes, width)), "ctx", 0, 0
    )

    gated = pl.pallas_call(
        gate_kernel,
        out_shape=jax.ShapeDtypeStruct((rows, width), BF16),
        in_specs=[pl.BlockSpec(memory_space=pltpu.SMEM)] + [whole] * 10,
        out_specs=whole,
        scratch_shapes=[
            pltpu.VMEM((width // LANES, rows, LANES), F32),
            pltpu.VMEM((modes, width), F32),
            pltpu.VMEM((width // LANES, rows, LANES), F32),
        ],
    )(
        ctx[None].astype(jnp.int32), query_input, key_input, value_input, halo, short_weight,
        residue, decay_rate, skip_gain[None], states, ends,
    )

    columns = out_weight.shape[1] // parts
    core_swap = [(i, i ^ 1) for i in range(parts)]

    def along_y(apart):
        return [(i, (i + 2 * apart) % parts) for i in range(parts)]

    def blocks_for(offsets, core):
        return (ch // 2 + jnp.array(offsets, jnp.int32)) % chips * 2 + core

    mine, partner = ch % 2, 1 - ch % 2
    sent_a = project(blocks_for((2, 1), partner), gated, out_weight, columns)
    got_a = lax.ppermute(sent_a, "ch", core_swap)
    sent_b = project(blocks_for((3, 0), partner), gated, out_weight, columns)
    got_b = lax.ppermute(sent_b, "ch", core_swap)
    far = project(blocks_for((2, 1), mine), gated, out_weight, columns, got_a)
    from2 = lax.ppermute(far[:rows], "ch", along_y(2))
    from1 = lax.ppermute(far[rows:], "ch", along_y(1))
    near = project(blocks_for((3, 0), mine), gated, out_weight, columns, got_b, F32)
    from3 = lax.ppermute(near[:rows].astype(BF16), "ch", along_y(3))
    total = (
        near[rows:] + from1.astype(F32) + from2.astype(F32) + from3.astype(F32)
    )
    return total.astype(BF16)


def solution(mesh):
    return jax.shard_map(
        body,
        mesh=mesh,
        in_specs=(
            P("ctx", "ch"),
            P("ctx", "ch"),
            P("ctx", "ch"),
            P(None, None, "ch"),
            P(None, "ch"),
            P(None, "ch"),
            P("ch"),
            P("ch", None),
        ),
        out_specs=P("ctx", "ch"),
        check_vma=False,
    )
```

```python
import functools

import jax
import jax.numpy as jnp
from jax import lax
from jax.experimental import pallas as pl
from jax.experimental.pallas import tpu as pltpu
from jax.sharding import PartitionSpec as P

F32 = jnp.float32
BF16 = jnp.bfloat16
SUBLANES = 8
LANES = 128


def rows_of(shape):
    return lax.broadcasted_iota(jnp.int32, shape, 0)


def short_conv(raw, prior, taps):
    x = raw.astype(F32)
    row = rows_of(x.shape)
    older = prior[0:1].astype(F32)
    newer = prior[1:2].astype(F32)
    back1 = jnp.where(row == 0, newer, pltpu.roll(x, 1, axis=0))
    back2 = jnp.where(
        row == 0, older, jnp.where(row == 1, newer, pltpu.roll(x, 2, axis=0))
    )
    return taps[0:1] * x + taps[1:2] * back1 + taps[2:3] * back2


def spread(row):
    return jnp.broadcast_to(row, (SUBLANES, row.shape[-1]))


def state_kernel(k_ref, v_ref, halo_ref, taps_ref, rate_ref, state_ref, ends_ref, mixed):
    modes, width = rate_ref.shape
    steps = k_ref.shape[0] // SUBLANES
    product = short_conv(k_ref[...], halo_ref[0:2], taps_ref[1]) * short_conv(
        v_ref[...], halo_ref[2:4], taps_ref[2]
    )
    for at in range(0, width, LANES):
        mixed[at // LANES] = product[:, at : at + LANES]
    left = (SUBLANES - 1 - rows_of((SUBLANES, LANES))).astype(F32) * float(steps)
    for at in range(0, width, LANES):
        cols = pl.ds(at, LANES)
        rate = rate_ref[:, cols]
        decay = jnp.exp(-rate)
        keep = [spread(decay[r : r + 1]) for r in range(modes)]
        held = [mixed[at // LANES, pl.ds(0, SUBLANES, steps), :]] * modes
        for a in range(1, steps):
            fresh = mixed[at // LANES, pl.ds(a, SUBLANES, steps), :]
            held = [keep[r] * held[r] + fresh for r in range(modes)]
        totals = []
        for r in range(modes):
            ends_ref[r, :, cols] = held[r]
            weight = jnp.exp(-spread(rate[r : r + 1]) * left)
            totals.append(jnp.sum(weight * held[r], axis=0, keepdims=True))
        state_ref[:, cols] = jnp.concatenate(totals, axis=0).astype(state_ref.dtype)


def gate_kernel(
    ctx_ref, q_ref, k_ref, v_ref, halo_ref, taps_ref, residue_ref, rate_ref, skip_ref,
    states_ref, ends_ref, gated_ref, mixed, carry, convolved,
):
    modes, width = rate_ref.shape
    rows = k_ref.shape[0]
    steps = rows // SUBLANES
    product = short_conv(k_ref[...], halo_ref[0:2], taps_ref[1]) * short_conv(
        v_ref[...], halo_ref[2:4], taps_ref[2]
    )
    for at in range(0, width, LANES):
        mixed[at // LANES] = product[:, at : at + LANES]
    across = jnp.exp(-rate_ref[...] * float(rows))

    def add_block(j, total):
        return across * total + states_ref[j].astype(F32)

    carry[...] = lax.fori_loop(0, ctx_ref[0], add_block, jnp.zeros((modes, width), F32))
    seg = rows_of((SUBLANES, LANES))
    for at in range(0, width, LANES):
        cols = pl.ds(at, LANES)
        rate = rate_ref[:, cols]
        decay = jnp.exp(-rate)
        skip1 = jnp.exp(-rate * float(steps))
        skip2 = skip1 * skip1
        skip4 = skip2 * skip2
        gain = residue_ref[:, cols] * jnp.sqrt(2.0 * rate)
        begin = carry[:, cols]
        held = []
        for r in range(modes):
            one = slice(r, r + 1)
            h = jnp.where(seg == 0, spread(begin[one]), pltpu.roll(ends_ref[r, :, cols], 1, axis=0))
            for apart, factor in ((1, skip1), (2, skip2), (4, skip4)):
                h = h + jnp.where(seg >= apart, spread(factor[one]), 0.0) * pltpu.roll(h, apart, axis=0)
            held.append(h)
        keep = [spread(decay[r : r + 1]) for r in range(modes)]
        gains = [spread(gain[r : r + 1]) for r in range(modes)]
        for a in range(steps):
            picked = pl.ds(a, SUBLANES, steps)
            fresh = mixed[at // LANES, picked, :]
            held = [keep[r] * held[r] + fresh for r in range(modes)]
            terms = [gains[r] * held[r] for r in range(modes)]
            while len(terms) > 1:
                terms = [x + y for x, y in zip(terms[::2], terms[1::2])]
            convolved[at // LANES, picked, :] = terms[0]
    query = short_conv(q_ref[...], halo_ref[4:6], taps_ref[0])
    for at in range(0, width, LANES):
        cols = pl.ds(at, LANES)
        long = convolved[at // LANES] + skip_ref[:, cols] * mixed[at // LANES]
        gated_ref[:, cols] = (query[:, at : at + LANES] * long).astype(gated_ref.dtype)


def start_weights(order_ref, weight_ref, held, arrived):
    chunk = held.shape[2]
    copies = []
    for i in range(held.shape[0]):
        columns = pl.ds(pl.multiple_of(order_ref[i] * chunk, chunk), chunk)
        copy = pltpu.make_async_copy(weight_ref.at[:, columns], held.at[i], arrived.at[i])
        copy.start()
        copies.append(copy)
    return copies


def project_chunks(copies, gated, held, outs):
    for i, copy in enumerate(copies):
        copy.wait()
        each = len(copies) // len(outs)
        out = outs[i // each]
        out[i % each] = jnp.dot(gated, held[i], preferred_element_type=F32).astype(out.dtype)


def gate_project_kernel(ctx_ref, order_ref, *refs):
    *inputs, weight_ref, gated_ref, first_ref, second_ref = refs[:14]
    mixed, carry, convolved, held, arrived = refs[14:]
    copies = start_weights(order_ref, weight_ref, held, arrived)
    gate_kernel(ctx_ref, *inputs, gated_ref, mixed, carry, convolved)
    project_chunks(copies, gated_ref[...], held, (first_ref, second_ref))


def project_kernel(order_ref, gated_ref, weight_ref, first_ref, second_ref, held, arrived):
    copies = start_weights(order_ref, weight_ref, held, arrived)
    project_chunks(copies, gated_ref[...], held, (first_ref, second_ref))


def first_sums_kernel(kept_ref, swapped_ref, to_a_ref, to_b_ref):
    for i in range(2):
        for out, at in ((to_a_ref, i), (to_b_ref, 2 + i)):
            out[i] = (kept_ref[at] + swapped_ref[at].astype(F32)).astype(out.dtype)


def second_sums_kernel(kept_ref, swapped_ref, from_ref, sum_ref, *, at):
    total = kept_ref[at] + swapped_ref[at].astype(F32) + from_ref[1].astype(F32)
    sum_ref[...] = total.astype(sum_ref.dtype)


def last_sums_kernel(kept_ref, swapped_ref, from_a_ref, from_b_ref, last_b_ref, last_a_ref, out_ref):
    chunk = kept_ref.shape[2]
    for half, (near, last) in enumerate(((from_a_ref, last_b_ref), (from_b_ref, last_a_ref))):
        at = 2 * half + 1
        total = kept_ref[at] + swapped_ref[at].astype(F32)
        total = total + near[0].astype(F32) + last[...].astype(F32)
        out_ref[:, half * chunk : (half + 1) * chunk] = total.astype(out_ref.dtype)


def body(
    query_input, key_input, value_input, short_weight, residue, decay_rate, skip_gain, out_weight
):
    ctx = lax.axis_index("ctx")
    blocks = lax.axis_size("ctx")
    ch = lax.axis_index("ch")
    parts = lax.axis_size("ch")
    chips = parts // 2
    rows, width = query_input.shape
    modes = residue.shape[0]
    last = rows - (short_weight.shape[1] - 1)
    edge = jnp.concatenate(
        [key_input[last:], value_input[last:], query_input[last:], query_input[last:]], axis=0
    )
    halo = lax.ppermute(edge, "ctx", [(i, i + 1) for i in range(blocks - 1)])

    whole = pl.BlockSpec(memory_space=pltpu.VMEM)
    state, ends = pl.pallas_call(
        state_kernel,
        out_shape=(
            jax.ShapeDtypeStruct((modes, width), BF16),
            jax.ShapeDtypeStruct((modes, SUBLANES, width), F32),
        ),
        in_specs=[whole] * 5,
        out_specs=(whole, whole),
        scratch_shapes=[pltpu.VMEM((width // LANES, rows, LANES), F32)],
    )(key_input, value_input, halo, short_weight, decay_rate)

    states = lax.all_to_all(
        jnp.broadcast_to(state[None], (blocks, modes, width)), "ctx", 0, 0
    )

    partner_core = [(i, i ^ 1) for i in range(parts)]
    pairing_a = [(i, (i // 2 ^ 1) * 2 + i % 2) for i in range(parts)]
    pairing_b = [(i, (chips - 1 - i // 2) * 2 + i % 2) for i in range(parts)]
    chip, core = ch // 2, ch % 2
    chip_a, chip_b, chip_c = chip ^ 1, chips - 1 - chip, (chips - 1 - chip) ^ 1
    chunk = out_weight.shape[1] // parts // 2

    def chunks_of(core):
        base = jnp.stack([chip_a, chip_c, chip_b, chip_c, chip_b, chip, chip_a, chip])
        half = jnp.array([0, 0, 1, 1, 0, 0, 1, 1], jnp.int32)
        return (base.astype(jnp.int32) * 2 + core) * 2 + half

    smem = pl.BlockSpec(memory_space=pltpu.SMEM)
    hbm = pl.BlockSpec(memory_space=pl.ANY)
    weights = [pltpu.VMEM((8, width, chunk), BF16), pltpu.SemaphoreType.DMA((8,))]

    def chunks_like(dtype):
        return jax.ShapeDtypeStruct((4, rows, chunk), dtype)

    gated, sent1, sent2 = pl.pallas_call(
        gate_project_kernel,
        out_shape=(jax.ShapeDtypeStruct((rows, width), BF16), chunks_like(BF16), chunks_like(BF16)),
        in_specs=[smem] * 2 + [whole] * 10 + [hbm],
        out_specs=(whole,) * 3,
        scratch_shapes=[
            pltpu.VMEM((width // LANES, rows, LANES), F32),
            pltpu.VMEM((modes, width), F32),
            pltpu.VMEM((width // LANES, rows, LANES), F32),
        ] + weights,
    )(
        ctx[None].astype(jnp.int32), chunks_of(1 - core), query_input, key_input, value_input,
        halo, short_weight, residue, decay_rate, skip_gain[None], states, ends, out_weight,
    )
    got1 = lax.ppermute(sent1, "ch", partner_core)
    got2 = lax.ppermute(sent2, "ch", partner_core)
    kept1, kept2 = pl.pallas_call(
        project_kernel,
        out_shape=(chunks_like(F32), chunks_like(F32)),
        in_specs=[smem, whole, hbm],
        out_specs=(whole,) * 2,
        scratch_shapes=weights,
        cost_estimate=pl.CostEstimate(
            flops=2 * rows * width * chunk * 8, bytes_accessed=16 * width * chunk, transcendentals=0
        ),
    )(chunks_of(core), gated, out_weight)
    half_pair = jax.ShapeDtypeStruct((2, rows, chunk), BF16)
    to_a, to_b = pl.pallas_call(
        first_sums_kernel, out_shape=(half_pair,) * 2, in_specs=[whole] * 2, out_specs=(whole,) * 2
    )(kept1, got1)
    from_a = lax.ppermute(to_a, "ch", pairing_a)
    from_b = lax.ppermute(to_b, "ch", pairing_b)

    def second_sum(near, at):
        return pl.pallas_call(
            functools.partial(second_sums_kernel, at=at),
            out_shape=jax.ShapeDtypeStruct((rows, chunk), BF16),
            in_specs=[whole] * 3,
            out_specs=whole,
        )(kept2, got2, near)

    last_b = lax.ppermute(second_sum(from_a, 0), "ch", pairing_b)
    last_a = lax.ppermute(second_sum(from_b, 2), "ch", pairing_a)
    return pl.pallas_call(
        last_sums_kernel,
        out_shape=jax.ShapeDtypeStruct((rows, 2 * chunk), BF16),
        in_specs=[whole] * 6,
        out_specs=whole,
    )(kept2, got2, from_a, from_b, last_b, last_a)


def solution(mesh):
    return jax.shard_map(
        body,
        mesh=mesh,
        in_specs=(
            P("ctx", "ch"),
            P("ctx", "ch"),
            P("ctx", "ch"),
            P(None, None, "ch"),
            P(None, "ch"),
            P(None, "ch"),
            P("ch"),
            P("ch", None),
        ),
        out_specs=P("ctx", "ch"),
        check_vma=False,
    )
```

```python
import functools

import jax
import jax.numpy as jnp
from jax import lax
from jax.experimental import pallas as pl
from jax.experimental.pallas import tpu as pltpu
from jax.sharding import PartitionSpec as P

F32 = jnp.float32
BF16 = jnp.bfloat16
SUBLANES = 8
LANES = 128
ROOM = pltpu.CompilerParams(vmem_limit_bytes=16 * 2**20)
SOME_ROOM = pltpu.CompilerParams(vmem_limit_bytes=50 * 2**20)


def rows_of(shape):
    return lax.broadcasted_iota(jnp.int32, shape, 0)


def short_conv(raw, prior, taps):
    x = raw.astype(F32)
    row = rows_of(x.shape)
    older = prior[0:1].astype(F32)
    newer = prior[1:2].astype(F32)
    back1 = jnp.where(row == 0, newer, pltpu.roll(x, 1, axis=0))
    back2 = jnp.where(
        row == 0, older, jnp.where(row == 1, newer, pltpu.roll(x, 2, axis=0))
    )
    return taps[0:1] * x + taps[1:2] * back1 + taps[2:3] * back2


def spread(row):
    return jnp.broadcast_to(row, (SUBLANES, row.shape[-1]))


def state_kernel(k_ref, v_ref, halo_ref, taps_ref, rate_ref, state_ref, ends_ref, mixed):
    modes, width = rate_ref.shape
    steps = k_ref.shape[0] // SUBLANES
    product = short_conv(k_ref[...], halo_ref[0:2], taps_ref[1]) * short_conv(
        v_ref[...], halo_ref[2:4], taps_ref[2]
    )
    for at in range(0, width, LANES):
        mixed[at // LANES] = product[:, at : at + LANES]
    left = (SUBLANES - 1 - rows_of((SUBLANES, LANES))).astype(F32) * float(steps)
    for at in range(0, width, LANES):
        cols = pl.ds(at, LANES)
        rate = rate_ref[:, cols]
        decay = jnp.exp(-rate)
        keep = [spread(decay[r : r + 1]) for r in range(modes)]
        held = [mixed[at // LANES, pl.ds(0, SUBLANES, steps), :]] * modes
        for a in range(1, steps):
            fresh = mixed[at // LANES, pl.ds(a, SUBLANES, steps), :]
            held = [keep[r] * held[r] + fresh for r in range(modes)]
        totals = []
        for r in range(modes):
            ends_ref[r, :, cols] = held[r]
            weight = jnp.exp(-spread(rate[r : r + 1]) * left)
            totals.append(jnp.sum(weight * held[r], axis=0, keepdims=True))
        state_ref[:, cols] = jnp.concatenate(totals, axis=0).astype(state_ref.dtype)


def gate_kernel(
    ctx_ref, q_ref, k_ref, v_ref, halo_ref, taps_ref, residue_ref, rate_ref, skip_ref,
    states_ref, ends_ref, gated_ref, mixed, carry, convolved,
):
    modes, width = rate_ref.shape
    rows = k_ref.shape[0]
    steps = rows // SUBLANES
    product = short_conv(k_ref[...], halo_ref[0:2], taps_ref[1]) * short_conv(
        v_ref[...], halo_ref[2:4], taps_ref[2]
    )
    for at in range(0, width, LANES):
        mixed[at // LANES] = product[:, at : at + LANES]
    across = jnp.exp(-rate_ref[...] * float(rows))

    def add_block(j, total):
        return across * total + states_ref[j].astype(F32)

    carry[...] = lax.fori_loop(0, ctx_ref[0], add_block, jnp.zeros((modes, width), F32))
    seg = rows_of((SUBLANES, LANES))
    for at in range(0, width, LANES):
        cols = pl.ds(at, LANES)
        rate = rate_ref[:, cols]
        decay = jnp.exp(-rate)
        skip1 = jnp.exp(-rate * float(steps))
        skip2 = skip1 * skip1
        skip4 = skip2 * skip2
        gain = residue_ref[:, cols] * jnp.sqrt(2.0 * rate)
        begin = carry[:, cols]
        held = []
        for r in range(modes):
            one = slice(r, r + 1)
            h = jnp.where(seg == 0, spread(begin[one]), pltpu.roll(ends_ref[r, :, cols], 1, axis=0))
            for apart, factor in ((1, skip1), (2, skip2), (4, skip4)):
                h = h + jnp.where(seg >= apart, spread(factor[one]), 0.0) * pltpu.roll(h, apart, axis=0)
            held.append(h)
        keep = [spread(decay[r : r + 1]) for r in range(modes)]
        gains = [spread(gain[r : r + 1]) for r in range(modes)]
        for a in range(steps):
            picked = pl.ds(a, SUBLANES, steps)
            fresh = mixed[at // LANES, picked, :]
            held = [keep[r] * held[r] + fresh for r in range(modes)]
            terms = [gains[r] * held[r] for r in range(modes)]
            while len(terms) > 1:
                terms = [x + y for x, y in zip(terms[::2], terms[1::2])]
            convolved[at // LANES, picked, :] = terms[0]
    query = short_conv(q_ref[...], halo_ref[4:6], taps_ref[0])
    for at in range(0, width, LANES):
        cols = pl.ds(at, LANES)
        long = convolved[at // LANES] + skip_ref[:, cols] * mixed[at // LANES]
        gated_ref[:, cols] = (query[:, at : at + LANES] * long).astype(gated_ref.dtype)


def start_weights(order_ref, weight_ref, held, arrived):
    chunk = held.shape[2]
    copies = []
    for i in range(held.shape[0]):
        columns = pl.ds(pl.multiple_of(order_ref[i] * chunk, chunk), chunk)
        copy = pltpu.make_async_copy(weight_ref.at[:, columns], held.at[i], arrived.at[i])
        copy.start()
        copies.append(copy)
    return copies


def project_chunks(copies, gated, held, outs):
    for i, copy in enumerate(copies):
        copy.wait()
        each = len(copies) // len(outs)
        out = outs[i // each]
        out[i % each] = jnp.dot(gated, held[i], preferred_element_type=F32).astype(out.dtype)


def gate_project_kernel(ctx_ref, order_ref, *refs):
    *inputs, weight_ref, gated_ref, first_ref, second_ref = refs[:14]
    mixed, carry, convolved, held, arrived = refs[14:]
    copies = start_weights(order_ref, weight_ref, held, arrived)
    gate_kernel(ctx_ref, *inputs, gated_ref, mixed, carry, convolved)
    project_chunks(copies, gated_ref[...], held, (first_ref, second_ref))


def project_kernel(order_ref, gated_ref, weight_ref, first_ref, second_ref, held, arrived):
    copies = start_weights(order_ref, weight_ref, held, arrived)
    project_chunks(copies, gated_ref[...], held, (first_ref, second_ref))


def first_sums_kernel(kept_ref, swapped_ref, to_a_ref, to_b_ref):
    for i in range(2):
        for out, at in ((to_a_ref, i), (to_b_ref, 2 + i)):
            out[i] = (kept_ref[at] + swapped_ref[at].astype(F32)).astype(out.dtype)


def second_sums_kernel(kept_ref, swapped_ref, from_ref, sum_ref, *, at):
    total = kept_ref[at] + swapped_ref[at].astype(F32) + from_ref[1].astype(F32)
    sum_ref[...] = total.astype(sum_ref.dtype)


def last_sums_kernel(kept_ref, swapped_ref, from_a_ref, from_b_ref, last_b_ref, last_a_ref, out_ref):
    chunk = kept_ref.shape[2]
    for half, (near, last) in enumerate(((from_a_ref, last_b_ref), (from_b_ref, last_a_ref))):
        at = 2 * half + 1
        total = kept_ref[at] + swapped_ref[at].astype(F32)
        total = total + near[0].astype(F32) + last[...].astype(F32)
        out_ref[:, half * chunk : (half + 1) * chunk] = total.astype(out_ref.dtype)


def body(
    query_input, key_input, value_input, short_weight, residue, decay_rate, skip_gain, out_weight
):
    ctx = lax.axis_index("ctx")
    blocks = lax.axis_size("ctx")
    ch = lax.axis_index("ch")
    parts = lax.axis_size("ch")
    chips = parts // 2
    rows, width = query_input.shape
    modes = residue.shape[0]
    last = rows - (short_weight.shape[1] - 1)
    edge = jnp.concatenate(
        [key_input[last:], value_input[last:], query_input[last:], query_input[last:]], axis=0
    )
    halo = lax.ppermute(edge, "ctx", [(i, i + 1) for i in range(blocks - 1)])

    whole = pl.BlockSpec(memory_space=pltpu.VMEM)
    state, ends = pl.pallas_call(
        state_kernel,
        out_shape=(
            jax.ShapeDtypeStruct((modes, width), BF16),
            jax.ShapeDtypeStruct((modes, SUBLANES, width), F32),
        ),
        in_specs=[whole] * 5,
        out_specs=(whole, whole),
        scratch_shapes=[pltpu.VMEM((width // LANES, rows, LANES), F32)],
    )(key_input, value_input, halo, short_weight, decay_rate)

    states = lax.all_to_all(
        jnp.broadcast_to(state[None], (blocks, modes, width)), "ctx", 0, 0
    )

    partner_core = [(i, i ^ 1) for i in range(parts)]
    pairing_a = [(i, (i // 2 ^ 1) * 2 + i % 2) for i in range(parts)]
    pairing_b = [(i, (chips - 1 - i // 2) * 2 + i % 2) for i in range(parts)]
    chip, core = ch // 2, ch % 2
    chip_a, chip_b, chip_c = chip ^ 1, chips - 1 - chip, (chips - 1 - chip) ^ 1
    chunk = out_weight.shape[1] // parts // 2

    def chunks_of(core):
        base = jnp.stack([chip_a, chip_c, chip_b, chip_c, chip_b, chip, chip_a, chip])
        half = jnp.array([0, 0, 1, 1, 0, 0, 1, 1], jnp.int32)
        return (base.astype(jnp.int32) * 2 + core) * 2 + half

    smem = pl.BlockSpec(memory_space=pltpu.SMEM)
    hbm = pl.BlockSpec(memory_space=pl.ANY)
    weights = [pltpu.VMEM((8, width, chunk), BF16), pltpu.SemaphoreType.DMA((8,))]

    def chunks_like(dtype):
        return jax.ShapeDtypeStruct((4, rows, chunk), dtype)

    gated, sent1, sent2 = pl.pallas_call(
        gate_project_kernel,
        out_shape=(jax.ShapeDtypeStruct((rows, width), BF16), chunks_like(BF16), chunks_like(BF16)),
        in_specs=[smem] * 2 + [whole] * 10 + [hbm],
        out_specs=(whole,) * 3,
        scratch_shapes=[
            pltpu.VMEM((width // LANES, rows, LANES), F32),
            pltpu.VMEM((modes, width), F32),
            pltpu.VMEM((width // LANES, rows, LANES), F32),
        ] + weights,
    )(
        ctx[None].astype(jnp.int32), chunks_of(1 - core), query_input, key_input, value_input,
        halo, short_weight, residue, decay_rate, skip_gain[None], states, ends, out_weight,
    )
    got1 = lax.ppermute(sent1, "ch", partner_core)
    got2 = lax.ppermute(sent2, "ch", partner_core)
    kept1, kept2 = pl.pallas_call(
        project_kernel,
        compiler_params=SOME_ROOM,
        out_shape=(chunks_like(F32), chunks_like(F32)),
        in_specs=[smem, whole, hbm],
        out_specs=(whole,) * 2,
        scratch_shapes=weights,
        cost_estimate=pl.CostEstimate(
            flops=2 * rows * width * chunk * 8, bytes_accessed=16 * width * chunk, transcendentals=0
        ),
    )(chunks_of(core), gated, out_weight)
    half_pair = jax.ShapeDtypeStruct((2, rows, chunk), BF16)
    to_a, to_b = pl.pallas_call(
        first_sums_kernel, compiler_params=ROOM, out_shape=(half_pair,) * 2, in_specs=[whole] * 2, out_specs=(whole,) * 2
    )(kept1, got1)
    from_a = lax.ppermute(to_a, "ch", pairing_a)
    from_b = lax.ppermute(to_b, "ch", pairing_b)

    def second_sum(near, at):
        return pl.pallas_call(
            functools.partial(second_sums_kernel, at=at),
            compiler_params=ROOM,
            out_shape=jax.ShapeDtypeStruct((rows, chunk), BF16),
            in_specs=[whole] * 3,
            out_specs=whole,
        )(kept2, got2, near)

    last_b = lax.ppermute(second_sum(from_a, 0), "ch", pairing_b)
    last_a = lax.ppermute(second_sum(from_b, 2), "ch", pairing_a)
    return pl.pallas_call(
        last_sums_kernel,
        compiler_params=ROOM,
        out_shape=jax.ShapeDtypeStruct((rows, 2 * chunk), BF16),
        in_specs=[whole] * 6,
        out_specs=whole,
    )(kept2, got2, from_a, from_b, last_b, last_a)


def solution(mesh):
    return jax.shard_map(
        body,
        mesh=mesh,
        in_specs=(
            P("ctx", "ch"),
            P("ctx", "ch"),
            P("ctx", "ch"),
            P(None, None, "ch"),
            P(None, "ch"),
            P(None, "ch"),
            P("ch"),
            P("ch", None),
        ),
        out_specs=P("ctx", "ch"),
        check_vma=False,
    )
```

```python
import functools

import jax
import jax.numpy as jnp
from jax import lax
from jax.experimental import pallas as pl
from jax.experimental.pallas import tpu as pltpu
from jax.sharding import PartitionSpec as P

F32 = jnp.float32
BF16 = jnp.bfloat16
SUBLANES = 8
LANES = 128
ROOM = pltpu.CompilerParams(vmem_limit_bytes=16 * 2**20)
SOME_ROOM = pltpu.CompilerParams(vmem_limit_bytes=50 * 2**20)


def rows_of(shape):
    return lax.broadcasted_iota(jnp.int32, shape, 0)


def short_conv(raw, prior, taps):
    x = raw.astype(F32)
    row = rows_of(x.shape)
    older = prior[0:1].astype(F32)
    newer = prior[1:2].astype(F32)
    back1 = jnp.where(row == 0, newer, pltpu.roll(x, 1, axis=0))
    back2 = jnp.where(
        row == 0, older, jnp.where(row == 1, newer, pltpu.roll(x, 2, axis=0))
    )
    return taps[0:1] * x + taps[1:2] * back1 + taps[2:3] * back2


def spread(row):
    return jnp.broadcast_to(row, (SUBLANES, row.shape[-1]))


def edge_kernel(k_ref, v_ref, q_ref, edge_ref, tails, arrived):
    rows, height = k_ref.shape[0], tails.shape[1]
    copies = [
        pltpu.make_async_copy(ref.at[pl.ds(rows - height, height), :], tails.at[i], arrived.at[i])
        for i, ref in enumerate((k_ref, v_ref, q_ref))
    ]
    for copy in copies:
        copy.start()
    for copy in copies:
        copy.wait()
    pieces = [tails[i].astype(F32)[height - 2 :] for i in (0, 1, 2, 2)]
    edge_ref[...] = jnp.concatenate(pieces, axis=0).astype(edge_ref.dtype)


def state_kernel(k_ref, v_ref, halo_ref, taps_ref, rate_ref, state_ref, ends_ref, mixed):
    modes, width = rate_ref.shape
    steps = k_ref.shape[0] // SUBLANES
    product = short_conv(k_ref[...], halo_ref[0:2], taps_ref[1]) * short_conv(
        v_ref[...], halo_ref[2:4], taps_ref[2]
    )
    for at in range(0, width, LANES):
        mixed[at // LANES] = product[:, at : at + LANES]
    left = (SUBLANES - 1 - rows_of((SUBLANES, LANES))).astype(F32) * float(steps)
    for at in range(0, width, LANES):
        cols = pl.ds(at, LANES)
        rate = rate_ref[:, cols]
        decay = jnp.exp(-rate)
        keep = [spread(decay[r : r + 1]) for r in range(modes)]
        held = [mixed[at // LANES, pl.ds(0, SUBLANES, steps), :]] * modes
        for a in range(1, steps):
            fresh = mixed[at // LANES, pl.ds(a, SUBLANES, steps), :]
            held = [keep[r] * held[r] + fresh for r in range(modes)]
        totals = []
        for r in range(modes):
            ends_ref[r, :, cols] = held[r]
            weight = jnp.exp(-spread(rate[r : r + 1]) * left)
            totals.append(jnp.sum(weight * held[r], axis=0, keepdims=True))
        total = jnp.concatenate(totals, axis=0).astype(state_ref.dtype)
        for j in range(state_ref.shape[0]):
            state_ref[j, :, cols] = total


def gate_kernel(
    ctx_ref, q_ref, k_ref, v_ref, halo_ref, taps_ref, residue_ref, rate_ref, skip_ref,
    states_ref, ends_ref, gated_ref, mixed, carry, convolved,
):
    modes, width = rate_ref.shape
    rows = k_ref.shape[0]
    steps = rows // SUBLANES
    product = short_conv(k_ref[...], halo_ref[0:2], taps_ref[1]) * short_conv(
        v_ref[...], halo_ref[2:4], taps_ref[2]
    )
    for at in range(0, width, LANES):
        mixed[at // LANES] = product[:, at : at + LANES]
    across = jnp.exp(-rate_ref[...] * float(rows))

    def add_block(j, total):
        return across * total + states_ref[j].astype(F32)

    carry[...] = lax.fori_loop(0, ctx_ref[0], add_block, jnp.zeros((modes, width), F32))
    seg = rows_of((SUBLANES, LANES))
    for at in range(0, width, LANES):
        cols = pl.ds(at, LANES)
        rate = rate_ref[:, cols]
        decay = jnp.exp(-rate)
        skip1 = jnp.exp(-rate * float(steps))
        skip2 = skip1 * skip1
        skip4 = skip2 * skip2
        gain = residue_ref[:, cols] * jnp.sqrt(2.0 * rate)
        begin = carry[:, cols]
        held = []
        for r in range(modes):
            one = slice(r, r + 1)
            h = jnp.where(seg == 0, spread(begin[one]), pltpu.roll(ends_ref[r, :, cols], 1, axis=0))
            for apart, factor in ((1, skip1), (2, skip2), (4, skip4)):
                h = h + jnp.where(seg >= apart, spread(factor[one]), 0.0) * pltpu.roll(h, apart, axis=0)
            held.append(h)
        keep = [spread(decay[r : r + 1]) for r in range(modes)]
        gains = [spread(gain[r : r + 1]) for r in range(modes)]
        for a in range(steps):
            picked = pl.ds(a, SUBLANES, steps)
            fresh = mixed[at // LANES, picked, :]
            held = [keep[r] * held[r] + fresh for r in range(modes)]
            terms = [gains[r] * held[r] for r in range(modes)]
            while len(terms) > 1:
                terms = [x + y for x, y in zip(terms[::2], terms[1::2])]
            convolved[at // LANES, picked, :] = terms[0]
    query = short_conv(q_ref[...], halo_ref[4:6], taps_ref[0])
    for at in range(0, width, LANES):
        cols = pl.ds(at, LANES)
        long = convolved[at // LANES] + skip_ref[:, cols] * mixed[at // LANES]
        gated_ref[:, cols] = (query[:, at : at + LANES] * long).astype(gated_ref.dtype)


def start_weights(order_ref, weight_ref, held, arrived):
    chunk = held.shape[2]
    copies = []
    for i in range(held.shape[0]):
        columns = pl.ds(pl.multiple_of(order_ref[i] * chunk, chunk), chunk)
        copy = pltpu.make_async_copy(weight_ref.at[:, columns], held.at[i], arrived.at[i])
        copy.start()
        copies.append(copy)
    return copies


def project_chunks(copies, gated, held, outs):
    for i, copy in enumerate(copies):
        copy.wait()
        each = len(copies) // len(outs)
        out = outs[i // each]
        out[i % each] = jnp.dot(gated, held[i], preferred_element_type=F32).astype(out.dtype)


def gate_project_kernel(ctx_ref, order_ref, *refs):
    *inputs, weight_ref, gated_ref, first_ref, second_ref = refs[:14]
    mixed, carry, convolved, held, arrived = refs[14:]
    copies = start_weights(order_ref, weight_ref, held, arrived)
    gate_kernel(ctx_ref, *inputs, gated_ref, mixed, carry, convolved)
    project_chunks(copies, gated_ref[...], held, (first_ref, second_ref))


def project_kernel(order_ref, gated_ref, weight_ref, first_ref, second_ref, held, arrived):
    copies = start_weights(order_ref, weight_ref, held, arrived)
    project_chunks(copies, gated_ref[...], held, (first_ref, second_ref))


def first_sums_kernel(kept_ref, swapped_ref, to_a_ref, to_b_ref):
    for i in range(2):
        for out, at in ((to_a_ref, i), (to_b_ref, 2 + i)):
            out[i] = (kept_ref[at] + swapped_ref[at].astype(F32)).astype(out.dtype)


def second_sums_kernel(kept_ref, swapped_ref, from_ref, sum_ref, *, at):
    total = kept_ref[at] + swapped_ref[at].astype(F32) + from_ref[1].astype(F32)
    sum_ref[...] = total.astype(sum_ref.dtype)


def last_sums_kernel(kept_ref, swapped_ref, from_a_ref, from_b_ref, last_b_ref, last_a_ref, out_ref):
    chunk = kept_ref.shape[2]
    for half, (near, last) in enumerate(((from_a_ref, last_b_ref), (from_b_ref, last_a_ref))):
        at = 2 * half + 1
        total = kept_ref[at] + swapped_ref[at].astype(F32)
        total = total + near[0].astype(F32) + last[...].astype(F32)
        out_ref[:, half * chunk : (half + 1) * chunk] = total.astype(out_ref.dtype)


def body(
    query_input, key_input, value_input, short_weight, residue, decay_rate, skip_gain, out_weight
):
    ctx = lax.axis_index("ctx")
    blocks = lax.axis_size("ctx")
    ch = lax.axis_index("ch")
    parts = lax.axis_size("ch")
    chips = parts // 2
    rows, width = query_input.shape
    modes = residue.shape[0]
    whole = pl.BlockSpec(memory_space=pltpu.VMEM)
    edge = pl.pallas_call(
        edge_kernel,
        out_shape=jax.ShapeDtypeStruct((SUBLANES, width), BF16),
        in_specs=[pl.BlockSpec(memory_space=pl.ANY)] * 3,
        out_specs=whole,
        scratch_shapes=[pltpu.VMEM((3, 16, width), BF16), pltpu.SemaphoreType.DMA((3,))],
    )(key_input, value_input, query_input)
    halo = lax.ppermute(edge, "ctx", [(i, i + 1) for i in range(blocks - 1)])

    state_copies, ends = pl.pallas_call(
        state_kernel,
        out_shape=(
            jax.ShapeDtypeStruct((blocks, modes, width), BF16),
            jax.ShapeDtypeStruct((modes, SUBLANES, width), F32),
        ),
        in_specs=[whole] * 5,
        out_specs=(whole, whole),
        scratch_shapes=[pltpu.VMEM((width // LANES, rows, LANES), F32)],
    )(key_input, value_input, halo, short_weight, decay_rate)

    states = lax.all_to_all(state_copies, "ctx", 0, 0)

    partner_core = [(i, i ^ 1) for i in range(parts)]
    pairing_a = [(i, (i // 2 ^ 1) * 2 + i % 2) for i in range(parts)]
    pairing_b = [(i, (chips - 1 - i // 2) * 2 + i % 2) for i in range(parts)]
    chip, core = ch // 2, ch % 2
    chip_a, chip_b, chip_c = chip ^ 1, chips - 1 - chip, (chips - 1 - chip) ^ 1
    chunk = out_weight.shape[1] // parts // 2

    def chunks_of(core):
        base = jnp.stack([chip_a, chip_c, chip_b, chip_c, chip_b, chip, chip_a, chip])
        half = jnp.array([0, 0, 1, 1, 0, 0, 1, 1], jnp.int32)
        return (base.astype(jnp.int32) * 2 + core) * 2 + half

    smem = pl.BlockSpec(memory_space=pltpu.SMEM)
    hbm = pl.BlockSpec(memory_space=pl.ANY)
    weights = [pltpu.VMEM((8, width, chunk), BF16), pltpu.SemaphoreType.DMA((8,))]

    def chunks_like(dtype):
        return jax.ShapeDtypeStruct((4, rows, chunk), dtype)

    gated, sent1, sent2 = pl.pallas_call(
        gate_project_kernel,
        out_shape=(jax.ShapeDtypeStruct((rows, width), BF16), chunks_like(BF16), chunks_like(BF16)),
        in_specs=[smem] * 2 + [whole] * 10 + [hbm],
        out_specs=(whole,) * 3,
        scratch_shapes=[
            pltpu.VMEM((width // LANES, rows, LANES), F32),
            pltpu.VMEM((modes, width), F32),
            pltpu.VMEM((width // LANES, rows, LANES), F32),
        ] + weights,
    )(
        ctx[None].astype(jnp.int32), chunks_of(1 - core), query_input, key_input, value_input,
        halo, short_weight, residue, decay_rate, skip_gain[None], states, ends, out_weight,
    )
    got1 = lax.ppermute(sent1, "ch", partner_core)
    got2 = lax.ppermute(sent2, "ch", partner_core)
    kept1, kept2 = pl.pallas_call(
        project_kernel,
        compiler_params=SOME_ROOM,
        out_shape=(chunks_like(F32), chunks_like(F32)),
        in_specs=[smem, whole, hbm],
        out_specs=(whole,) * 2,
        scratch_shapes=weights,
        cost_estimate=pl.CostEstimate(
            flops=2 * rows * width * chunk * 8, bytes_accessed=16 * width * chunk, transcendentals=0
        ),
    )(chunks_of(core), gated, out_weight)
    half_pair = jax.ShapeDtypeStruct((2, rows, chunk), BF16)
    to_a, to_b = pl.pallas_call(
        first_sums_kernel, compiler_params=ROOM, out_shape=(half_pair,) * 2, in_specs=[whole] * 2, out_specs=(whole,) * 2
    )(kept1, got1)
    from_a = lax.ppermute(to_a, "ch", pairing_a)
    from_b = lax.ppermute(to_b, "ch", pairing_b)

    def second_sum(near, at):
        return pl.pallas_call(
            functools.partial(second_sums_kernel, at=at),
            compiler_params=ROOM,
            out_shape=jax.ShapeDtypeStruct((rows, chunk), BF16),
            in_specs=[whole] * 3,
            out_specs=whole,
        )(kept2, got2, near)

    last_b = lax.ppermute(second_sum(from_a, 0), "ch", pairing_b)
    last_a = lax.ppermute(second_sum(from_b, 2), "ch", pairing_a)
    return pl.pallas_call(
        last_sums_kernel,
        compiler_params=ROOM,
        out_shape=jax.ShapeDtypeStruct((rows, 2 * chunk), BF16),
        in_specs=[whole] * 6,
        out_specs=whole,
    )(kept2, got2, from_a, from_b, last_b, last_a)


def solution(mesh):
    return jax.shard_map(
        body,
        mesh=mesh,
        in_specs=(
            P("ctx", "ch"),
            P("ctx", "ch"),
            P("ctx", "ch"),
            P(None, None, "ch"),
            P(None, "ch"),
            P(None, "ch"),
            P("ch"),
            P("ch", None),
        ),
        out_specs=P("ctx", "ch"),
        check_vma=False,
    )
```
